32 devices in a mesh: groups: 2 (over y), seq: 4 (over z), head: 4 (over x, core).
Axes of the slice: x: 2, y: 2, z: 4, core: 2. Of those that a mesh axis runs over, the one named last changes fastest.
Arguments:
- queries: bfloat16 [32, 3, 32, 128], P('groups', None, 'head'), parts along dimension 0, may hold values from -8 to 8
- new_kv: bfloat16 [4, 16, 3, 4, 128], P('groups', None, None, 'head'), parts along dimension 0, may hold values from -16 to 16
- res_kv: bfloat16 [4, 2, 16384, 4, 128], P('groups', None, 'seq', 'head'), parts along dimension 0, may hold values from -16 to 16
- prefill_kv: bfloat16 [4, 4, 4096, 128], P('groups', None, ('seq', 'head')), parts along dimension 0, may hold values from -16 to 16
- block_table: int32 [128], P('groups'), parts along dimension 0, may hold values from 0 to 63, as said below
- lengths: int32 [6], P('groups'), parts along dimension 0, may hold values from 4096 to 16384, as said below
- join_step: int32 [2], P('groups'), parts along dimension 0, may hold values from 1 to 15
Outputs:
- attn_out: bfloat16 [32, 3, 32, 128], P('groups', None, 'head'), parts along dimension 0
- new_cache: bfloat16 [4, 4, 4096, 128], P('groups', 'head', 'seq'), parts along dimension 0
The draws below stay inside these ranges and needn't reach their ends.
There are 2 independent parts, one for each index of `groups`. The reference program is written for one: setup_inputs(seed, part) draws one part's arguments, and reference() takes and returns one part's arrays. A program takes and returns all parts, laid end to end along the dimension named above; each array names one. Nothing has to cross between parts.
Inputs may be any that keep to these rules, and one draw needn't show every extreme that they name: `block_table`: A permutation of 0 to 63. In each aligned run of 4 entries (the blocks of one prefill device) every aligned range of 16 slots is named exactly 1 times. `lengths`: entries 0 to 1 lie between 4096 and 16384, and one of them equals 16384; entry 2 equals 4096.
All inputs are finite; a program needn't handle non-finite values.
Results may differ from the reference program's by a relative error of at most 0.0039.
Values may be sent and summed in bfloat16 or wider, within the bound.
No kernel may reach another device: no remote copies, remote signals or barrier semaphores. Data moves between devices by JAX's collectives and lax.ppermute only.
A program may use at most 64 MiB of HBM per device.

```python
import math
import jax
import jax.numpy as jnp
from jax import lax

HD = 128
QPK = 8
RES = 2
STEPS = 16
BLOCK = 64
PAGES = 1
KVH = 4
QH = 32
DEV_BLOCKS = 4
LNEW = 4096
NBLK = 64
RES_LEN = 16384


def query_values(key):
    array_shape = (STEPS, RES + 1, QH, HD)
    base_draw = jax.random.normal(jax.random.fold_in(key, 31), array_shape, jnp.float32)
    return jnp.clip(base_draw, -8.0, 8.0)


def draw_queries(key, part):
    return query_values(key).astype(jnp.bfloat16)


def draw_new_kv(key, part):
    array_shape = (STEPS, RES + 1, KVH, HD)
    centre = query_values(key).reshape(STEPS, RES + 1, KVH, QPK, HD).mean(axis=3)
    key_part = 9.0 * centre + 1.5 * jax.random.normal(jax.random.fold_in(key, 51), array_shape, jnp.float32)
    value_part = jax.random.normal(jax.random.fold_in(key, 52), array_shape, jnp.float32)
    return jnp.clip(jnp.stack([key_part, value_part]), -16.0, 16.0).astype(jnp.bfloat16)


def draw_res_kv(key, part):
    array_shape = (RES, RES_LEN, KVH, HD)
    key_part = 3.0 * jax.random.normal(jax.random.fold_in(key, 11), array_shape, jnp.float32)
    value_part = jax.random.normal(jax.random.fold_in(key, 12), array_shape, jnp.float32)
    return jnp.clip(jnp.stack([key_part, value_part]), -16.0, 16.0).astype(jnp.bfloat16)


def draw_prefill_kv(key, part):
    array_shape = (KVH, LNEW, HD)
    key_part = 3.0 * jax.random.normal(jax.random.fold_in(key, 13), array_shape, jnp.float32)
    value_part = jax.random.normal(jax.random.fold_in(key, 14), array_shape, jnp.float32)
    return jnp.clip(jnp.stack([key_part, value_part]), -16.0, 16.0).astype(jnp.bfloat16)


def shuffle_pattern(sub_key, pattern):
    return jax.random.permutation(sub_key, pattern)


def draw_block_table(key, part):
    shard_count = DEV_BLOCKS // PAGES
    sender_count = NBLK // DEV_BLOCKS
    pattern = jnp.repeat(jnp.arange(shard_count, dtype=jnp.int32), PAGES)
    sender_keys = jax.random.split(jax.random.fold_in(key, 41), sender_count)
    shard_of = jax.vmap(shuffle_pattern, in_axes=(0, None))(sender_keys, pattern).reshape(-1).astype(jnp.int32)
    priority = jax.random.permutation(jax.random.fold_in(key, 42), NBLK).astype(jnp.int32)
    ordering = jnp.argsort(shard_of * NBLK + priority, stable=True).astype(jnp.int32)
    return jnp.zeros((NBLK,), jnp.int32).at[ordering].set(jnp.arange(NBLK, dtype=jnp.int32))


def draw_lengths(key, part):
    resident = jax.random.randint(jax.random.fold_in(key, 61), (RES,), RES_LEN // 4, RES_LEN + 1)
    full_one = jax.random.randint(jax.random.fold_in(key, 63), (), 0, RES)
    resident = jnp.where(jnp.arange(RES, dtype=jnp.int32) == full_one, RES_LEN, resident)
    joining = jnp.full((1,), LNEW, jnp.int32)
    return jnp.concatenate([resident.astype(jnp.int32), joining]).astype(jnp.int32)


def setup_inputs(seed: int = 0, part: int = 0) -> dict:
    key_of = jax.random.split(jax.random.key(seed), 8)
    part_keys = jax.random.split(jax.random.fold_in(key_of[7], part), 8)
    return {
        "queries": draw_queries(jax.random.fold_in(jax.random.fold_in(key_of[7], part), 71), part),
        "new_kv": draw_new_kv(jax.random.fold_in(jax.random.fold_in(key_of[7], part), 71), part),
        "res_kv": draw_res_kv(jax.random.fold_in(jax.random.fold_in(key_of[7], part), 71), part),
        "prefill_kv": draw_prefill_kv(jax.random.fold_in(jax.random.fold_in(key_of[7], part), 71), part),
        "block_table": draw_block_table(jax.random.fold_in(jax.random.fold_in(key_of[7], part), 71), part),
        "lengths": draw_lengths(jax.random.fold_in(jax.random.fold_in(key_of[7], part), 71), part),
        "join_step": jax.random.randint(part_keys[6], (1,), 1, STEPS).astype(jnp.int32),
    }


def attend(query_rows, head_keys, head_values, valid_mask, fresh_keys, fresh_values, fresh_valid):
    score_scale = 1.0 / math.sqrt(HD)
    highest = lax.Precision.HIGHEST

    def per_head(operands):
        rows_here, keys_here, values_here, new_keys, new_values = operands
        rows_wide = rows_here.astype(jnp.float32)
        cache_scores = jnp.einsum('sqd,ld->sql', rows_wide, keys_here.astype(jnp.float32), precision=highest) * score_scale
        cache_scores = jnp.where(valid_mask[None, None, :], cache_scores, -jnp.inf)
        fresh_scores = jnp.einsum('sqd,ud->squ', rows_wide, new_keys.astype(jnp.float32), precision=highest) * score_scale
        fresh_scores = jnp.where(fresh_valid[:, None, :], fresh_scores, -jnp.inf)
        row_max = jnp.maximum(lax.optimization_barrier(jnp.max(cache_scores, axis=-1)), lax.optimization_barrier(jnp.max(fresh_scores, axis=-1)))
        cache_weight = jnp.exp(cache_scores - row_max[..., None])
        fresh_weight = jnp.exp(fresh_scores - row_max[..., None])
        row_total = lax.optimization_barrier(jnp.sum(cache_weight, axis=-1)) + lax.optimization_barrier(jnp.sum(fresh_weight, axis=-1))
        cache_round = lax.optimization_barrier(cache_weight.astype(jnp.bfloat16)).astype(jnp.float32)
        fresh_round = lax.optimization_barrier(fresh_weight.astype(jnp.bfloat16)).astype(jnp.float32)
        summed = jnp.einsum('sql,ld->sqd', cache_round, values_here.astype(jnp.float32), precision=highest)
        summed = summed + jnp.einsum('squ,ud->sqd', fresh_round, new_values.astype(jnp.float32), precision=highest)
        return summed / row_total[..., None]
    answer = lax.map(per_head, (jnp.transpose(query_rows, (1, 0, 2, 3)), head_keys, head_values, jnp.transpose(fresh_keys, (1, 0, 2)), jnp.transpose(fresh_values, (1, 0, 2))))
    return jnp.transpose(answer, (1, 0, 2, 3)).reshape(STEPS, KVH * QPK, HD)

def reference(queries, new_kv, res_kv, prefill_kv, block_table, lengths, join_step):
    joined = join_step[0]
    step_ids = jnp.arange(STEPS, dtype=jnp.int32)
    earlier = step_ids[None, :] <= step_ids[:, None]
    answers = []
    for request in range(RES):
        valid_mask = jnp.arange(RES_LEN, dtype=jnp.int32) < lengths[request]
        query_rows = queries[:, request].reshape(STEPS, KVH, QPK, HD)
        head_keys = jnp.moveaxis(res_kv[0, request], 1, 0)
        head_values = jnp.moveaxis(res_kv[1, request], 1, 0)
        answers.append(attend(query_rows, head_keys, head_values, valid_mask, new_kv[0, :, request], new_kv[1, :, request], earlier))
    valid_mask = jnp.arange(LNEW, dtype=jnp.int32) < lengths[RES]
    query_rows = queries[:, RES].reshape(STEPS, KVH, QPK, HD)
    fresh_valid = earlier & (step_ids[None, :] >= joined)
    joining = attend(query_rows, prefill_kv[0], prefill_kv[1], valid_mask, new_kv[0, :, RES], new_kv[1, :, RES], fresh_valid)
    joining = jnp.where((step_ids >= joined)[:, None, None], joining, 0.0)
    attn_out = jnp.stack(answers + [joining], axis=1).astype(jnp.bfloat16)
    blocks = prefill_kv.reshape(2, KVH, NBLK, BLOCK, HD)
    new_cache = jnp.zeros_like(blocks).at[:, :, block_table].set(blocks).reshape(2, KVH, LNEW, HD)
    return (attn_out, new_cache)
```

```python
import functools
import math

import jax
import jax.numpy as jnp
from jax import lax
from jax.experimental import pallas as pl
from jax.experimental.pallas import tpu as pltpu
from jax.sharding import PartitionSpec as P

FLOOR = -1e30
MASKED = -2e30
PIECES = 3
LOG2E = math.log2(math.e)


def vmem():
    return pl.BlockSpec(memory_space=pltpu.VMEM)


def smem():
    return pl.BlockSpec(memory_space=pltpu.SMEM)


def anywhere():
    return pl.BlockSpec(memory_space=pl.ANY)


def query_rows(q_ref, request):
    steps, _, group, depth = q_ref.shape
    wide = q_ref[:, request].astype(jnp.float32)
    return wide.reshape(steps * group, depth).astype(jnp.bfloat16)


def empty_state(rows, depth):
    return (
        jnp.full((rows, 1), FLOOR, jnp.float32),
        jnp.zeros((rows, 1), jnp.float32),
        jnp.zeros((rows, depth), jnp.float32),
    )


def absorb(state, query, keys, values, scale, bias):
    row_max, total, summed = state
    scores = lax.dot_general(
        query, keys, (((1,), (1,)), ((), ())), preferred_element_type=jnp.float32
    )
    scores = scores * scale
    if bias is not None:
        scores = scores + bias
    new_max = jnp.maximum(row_max, jnp.max(scores, axis=1, keepdims=True))
    fade = jnp.exp2(row_max - new_max)
    weight = jnp.exp2(scores - new_max)
    total = total * fade + jnp.sum(weight, axis=1, keepdims=True)
    summed = summed * fade + jnp.dot(
        weight.astype(jnp.bfloat16), values, preferred_element_type=jnp.float32
    )
    return new_max, total, summed


def fresh_bias(steps, group, request, resident, joined, owner):
    rows = steps * group
    row_step = lax.broadcasted_iota(jnp.int32, (rows, steps), 0) // group
    key_step = lax.broadcasted_iota(jnp.int32, (rows, steps), 1)
    allowed = (key_step <= row_step) & owner
    if request >= resident:
        allowed = allowed & (key_step >= joined)
    return jnp.where(allowed, 0.0, MASKED)


def unit(rows):
    return lax.broadcasted_iota(jnp.int32, (rows, rows), 0) == lax.broadcasted_iota(
        jnp.int32, (rows, rows), 1
    )


def to_row(column, diagonal):
    return jnp.sum(jnp.where(diagonal, column, 0.0), axis=0, keepdims=True)


def to_column(row, diagonal):
    return jnp.sum(jnp.where(diagonal, row, 0.0), axis=1, keepdims=True)


def split(row):
    parts = []
    rest = row
    for _ in range(PIECES):
        part = rest.astype(jnp.bfloat16).astype(jnp.float32)
        parts.append(part)
        rest = rest - part
    return parts


def finish(state, diagonal):
    row_max, total, summed = state
    safe = jnp.where(total > 0.0, total, 1.0)
    return summed / safe, to_row(row_max + jnp.log2(safe), diagonal)


def tail_rows(levels):
    parts = [part for level in levels for part in split(level)]
    width = parts[0].shape[1]
    count = -(-len(parts) // 16) * 16
    parts.append(jnp.zeros((count - len(parts), width), jnp.float32))
    return jnp.concatenate(parts, axis=0).astype(jnp.bfloat16)


def pack_kernel(slots, table_ref, place_ref, block_ref, send_ref):
    _, heads, dev_blocks, _, _ = block_ref.shape
    for block in range(dev_blocks):
        shard = table_ref[place_ref[0] * dev_blocks + block] // slots
        for head in range(heads):
            for part in range(2):
                send_ref[shard * heads + head, part] = block_ref[part, head, block]


def resident_kernel(
    scale, chunk, len_ref, place_ref, q_ref, fresh_ref, kv_hbm, out_ref, level_ref, kv_ref, sems
):
    resident, length = kv_hbm.shape[1], kv_hbm.shape[2]
    steps, _, group, depth = q_ref.shape
    rows = steps * group
    count = length // chunk

    def copy(request, index, part):
        window = pl.ds(index * chunk, chunk)
        return pltpu.make_async_copy(
            kv_hbm.at[part, request, window],
            kv_ref.at[part, request, window],
            sems.at[part, request, index],
        )

    for request in range(resident):
        for index in range(count):
            for part in range(2):
                copy(request, index, part).start()
    diagonal = unit(rows)
    seq_index = place_ref[1]
    owner = seq_index == 0
    for request in range(resident):
        query = query_rows(q_ref, request)
        state = absorb(
            empty_state(rows, depth),
            query,
            fresh_ref[0, request],
            fresh_ref[1, request],
            scale,
            fresh_bias(steps, group, request, resident, 0, owner),
        )
        for index in range(count):
            copy(request, index, 0).wait()
            copy(request, index, 1).wait()
            start = seq_index * length + index * chunk
            position = start + lax.broadcasted_iota(jnp.int32, (1, chunk), 1)
            bias = jnp.where(position < len_ref[request], 0.0, MASKED)
            window = pl.ds(index * chunk, chunk)
            state = absorb(
                state, query, kv_ref[0, request, window], kv_ref[1, request, window], scale, bias
            )
        mean, level = finish(state, diagonal)
        out_ref[pl.ds(request * rows, rows), :] = mean.astype(jnp.bfloat16)
        level_ref[pl.ds(request, 1), :] = level


def place_kernel(
    scale,
    chunk,
    table_ref,
    place_ref,
    join_ref,
    q_ref,
    fresh_ref,
    arrived_ref,
    res_ref,
    res_level_ref,
    cache_ref,
    pay_ref,
):
    senders = arrived_ref.shape[0]
    _, slots, block_len, depth = cache_ref.shape
    dev_blocks = table_ref.shape[0] // senders
    steps, requests, group, _ = q_ref.shape
    rows = steps * group
    resident = requests - 1
    seq_index = place_ref[1]
    base = seq_index * slots

    def settle(sender, carry):
        def look(block, found):
            slot = table_ref[sender * dev_blocks + block] - base
            return jnp.where((slot >= 0) & (slot < slots), slot, found)

        found = lax.fori_loop(0, dev_blocks, look, 0, unroll=True)
        for part in range(2):
            cache_ref[part, found] = arrived_ref[sender, part]
        return carry

    lax.fori_loop(0, senders, settle, 0)
    diagonal = unit(rows)
    query = query_rows(q_ref, resident)
    state = absorb(
        empty_state(rows, depth),
        query,
        fresh_ref[0, resident],
        fresh_ref[1, resident],
        scale,
        fresh_bias(steps, group, resident, resident, join_ref[0], seq_index == 0),
    )
    per_chunk = chunk // block_len
    for index in range(senders // per_chunk):
        window = pl.ds(index * per_chunk, per_chunk)
        keys = arrived_ref[window, 0].reshape(chunk, depth)
        values = arrived_ref[window, 1].reshape(chunk, depth)
        state = absorb(state, query, keys, values, scale, None)
    mean, level = finish(state, diagonal)
    pay_ref[pl.ds(0, resident * rows), :] = res_ref[...]
    pay_ref[pl.ds(resident * rows, rows), :] = mean.astype(jnp.bfloat16)
    levels = [res_level_ref[pl.ds(request, 1), :] for request in range(resident)] + [level]
    pay_ref[pl.ds(requests * rows, 16), :] = tail_rows(levels)


def merged(flag, mine_ref, other_ref, request, requests, rows, diagonal):
    def ordered(window):
        mine = mine_ref[window, :].astype(jnp.float32)
        other = other_ref[window, :].astype(jnp.float32)
        return jnp.where(flag, mine, other), jnp.where(flag, other, mine)

    first_tail, second_tail = ordered(pl.ds(requests * rows, 16))

    def level_of(tail):
        level = tail[request * PIECES : request * PIECES + 1]
        for piece in range(1, PIECES):
            at = request * PIECES + piece
            level = level + tail[at : at + 1]
        return level

    first_level, second_level = level_of(first_tail), level_of(second_tail)
    top = jnp.maximum(first_level, second_level)
    first_weight = jnp.exp2(first_level - top)
    second_weight = jnp.exp2(second_level - top)
    total = first_weight + second_weight
    first_share = to_column(first_weight / total, diagonal)
    second_share = to_column(second_weight / total, diagonal)
    first, second = ordered(pl.ds(request * rows, rows))
    return first * first_share + second * second_share, top + jnp.log2(total)


def merge_kernel(requests, flag_ref, mine_ref, other_ref, out_ref):
    rows = mine_ref.shape[1]
    flag = flag_ref[0] == 0
    diagonal = unit(rows)
    levels = []
    for request in range(requests):
        mean, level = merged(flag, mine_ref, other_ref, request, requests, rows, diagonal)
        out_ref[pl.ds(request * rows, rows), :] = mean.astype(jnp.bfloat16)
        levels.append(level)
    out_ref[pl.ds(requests * rows, 16), :] = tail_rows(levels)


def final_kernel(flag_ref, join_ref, mine_ref, other_ref, out_ref):
    steps, requests, group, depth = out_ref.shape
    rows = mine_ref.shape[1]
    flag = flag_ref[0] == 0
    diagonal = unit(rows)
    for request in range(requests):
        mean, _ = merged(flag, mine_ref, other_ref, request, requests, rows, diagonal)
        if request == requests - 1:
            step = lax.broadcasted_iota(jnp.int32, (rows, depth), 0) // group
            mean = jnp.where(step >= join_ref[0], mean, 0.0)
        out_ref[:, request] = mean.reshape(steps, group, depth).astype(jnp.bfloat16)


def call(kernel, out_shape, in_specs, out_specs, cost, scratch=()):
    return pl.pallas_call(
        kernel,
        out_shape=out_shape,
        in_specs=in_specs,
        out_specs=out_specs,
        scratch_shapes=list(scratch),
        cost_estimate=pl.CostEstimate(flops=cost, bytes_accessed=cost // 128, transcendentals=0),
    )


def per_device(queries, new_kv, res_kv, prefill_kv, block_table, lengths, join_step):
    seq_index = lax.axis_index("seq")
    head_index = lax.axis_index("head")
    seq_count = lax.axis_size("seq")
    head_count = lax.axis_size("head")
    senders = seq_count * head_count
    steps, requests, group, depth = queries.shape
    rows = steps * group
    resident = res_kv.shape[1]
    res_rows = res_kv.shape[2]
    head_total = prefill_kv.shape[1]
    total_blocks = block_table.shape[0]
    dev_blocks = total_blocks // senders
    block_len = prefill_kv.shape[2] // dev_blocks
    slots = total_blocks // seq_count
    assert dev_blocks == seq_count and head_total == head_count and rows == depth
    assert seq_count & (seq_count - 1) == 0
    scale = LOG2E / math.sqrt(depth)
    bf16, f32 = jnp.bfloat16, jnp.float32
    place = jnp.stack([seq_index * head_count + head_index, seq_index]).astype(jnp.int32)
    blocks = prefill_kv.reshape(2, head_total, dev_blocks, block_len, depth)
    fresh = jnp.transpose(new_kv[:, :, :, 0], (0, 2, 1, 3))

    outgoing = call(
        functools.partial(pack_kernel, slots),
        jax.ShapeDtypeStruct((senders, 2, block_len, depth), bf16),
        [smem(), smem(), vmem()],
        vmem(),
        1 << 20,
    )(block_table, place, blocks)
    arrived = lax.all_to_all(outgoing, ("seq", "head"), split_axis=0, concat_axis=0, tiled=True)

    chunk = min(1024, res_rows)
    res_mean, res_level = call(
        functools.partial(resident_kernel, scale, chunk),
        (
            jax.ShapeDtypeStruct((resident * rows, depth), bf16),
            jax.ShapeDtypeStruct((resident, rows), f32),
        ),
        [smem(), smem(), vmem(), vmem(), anywhere()],
        (vmem(), vmem()),
        4 * resident * rows * res_rows * depth,
        [
            pltpu.VMEM((2, resident, res_rows, depth), bf16),
            pltpu.SemaphoreType.DMA((2, resident, res_rows // chunk)),
        ],
    )(lengths, place, queries, fresh, res_kv[:, :, :, 0])

    pay_shape = jax.ShapeDtypeStruct((requests * rows + 16, depth), bf16)
    cache, payload = call(
        functools.partial(place_kernel, scale, min(1024, senders * block_len)),
        (jax.ShapeDtypeStruct((2, slots, block_len, depth), bf16), pay_shape),
        [smem(), smem(), smem(), vmem(), vmem(), vmem(), vmem(), vmem()],
        (vmem(), vmem()),
        4 * rows * senders * block_len * depth,
    )(block_table, place, join_step, queries, fresh, arrived, res_mean, res_level)
    new_cache = cache.reshape(2, 1, slots * block_len, depth)

    bit = 1
    while bit < seq_count:
        pairs = [(index, index ^ bit) for index in range(seq_count)]
        other = lax.ppermute(payload, "seq", pairs)
        flag = ((seq_index // bit) % 2).astype(jnp.int32).reshape(1)
        bit *= 2
        if bit < seq_count:
            payload = call(
                functools.partial(merge_kernel, requests),
                pay_shape,
                [smem(), vmem(), vmem()],
                vmem(),
                1 << 20,
            )(flag, payload, other)
    attn_out = call(
        final_kernel,
        jax.ShapeDtypeStruct((steps, requests, group, depth), bf16),
        [smem(), smem(), vmem(), vmem()],
        vmem(),
        1 << 20,
    )(flag, join_step, payload, other)
    return (attn_out, new_cache)


def solution(mesh):
    in_specs = (
        P("groups", None, "head", None),
        P("groups", None, None, "head", None),
        P("groups", None, "seq", "head", None),
        P("groups", None, ("seq", "head"), None),
        P("groups"),
        P("groups"),
        P("groups"),
    )
    out_specs = (P("groups", None, "head", None), P("groups", "head", "seq", None))
    return jax.shard_map(
        per_device, mesh=mesh, in_specs=in_specs, out_specs=out_specs, check_vma=False
    )
```

```python
import functools
import math

import jax
import jax.numpy as jnp
from jax import lax
from jax.experimental import pallas as pl
from jax.experimental.pallas import tpu as pltpu
from jax.sharding import PartitionSpec as P

FLOOR = -1e30
MASKED = -2e30
PIECES = 3
LOG2E = math.log2(math.e)


def vmem():
    return pl.BlockSpec(memory_space=pltpu.VMEM)


def smem():
    return pl.BlockSpec(memory_space=pltpu.SMEM)


def query_rows(q_ref, request):
    steps, _, group, depth = q_ref.shape
    wide = q_ref[:, request].astype(jnp.float32)
    return wide.reshape(steps * group, depth).astype(jnp.bfloat16)


def fresh_bias(steps, group, request, resident, joined, owner):
    rows = steps * group
    row_step = lax.broadcasted_iota(jnp.int32, (rows, steps), 0) // group
    key_step = lax.broadcasted_iota(jnp.int32, (rows, steps), 1)
    allowed = (key_step <= row_step) & owner
    if request >= resident:
        allowed = allowed & (key_step >= joined)
    return jnp.where(allowed, 0.0, MASKED)


def unit(rows):
    return lax.broadcasted_iota(jnp.int32, (rows, rows), 0) == lax.broadcasted_iota(
        jnp.int32, (rows, rows), 1
    )


def to_row(column, diagonal):
    return jnp.sum(jnp.where(diagonal, column, 0.0), axis=0, keepdims=True)


def to_column(row, diagonal):
    return jnp.sum(jnp.where(diagonal, row, 0.0), axis=1, keepdims=True)


def split(row):
    parts = []
    rest = row
    for _ in range(PIECES):
        part = rest.astype(jnp.bfloat16).astype(jnp.float32)
        parts.append(part)
        rest = rest - part
    return parts


def finish(state, diagonal):
    row_max, total, summed = state
    safe = jnp.where(total > 0.0, total, 1.0)
    return summed / safe, to_row(row_max + jnp.log2(safe), diagonal)


def tail_rows(levels):
    parts = [part for level in levels for part in split(level)]
    width = parts[0].shape[1]
    count = -(-len(parts) // 16) * 16
    parts.append(jnp.zeros((count - len(parts), width), jnp.float32))
    return jnp.concatenate(parts, axis=0).astype(jnp.bfloat16)


def lanes(wide, op):
    width = wide.shape[1]
    step = min(width, 128)
    out = wide[:, :step]
    for start in range(step, width, step):
        out = op(out, wide[:, start : start + step])
    return out


def attend(query, parts, scale, score_ref, copies=()):
    if copies:
        copies[0].wait()
    rows = query.shape[0]
    top = None
    start = 0
    for keys, _, bias in parts:
        count = keys.shape[0]
        scores = lax.dot_general(
            query, keys[...], (((1,), (1,)), ((), ())), preferred_element_type=jnp.float32
        )
        scores = scores * scale
        if bias is not None:
            scores = scores + bias
        score_ref[:, pl.ds(start, count)] = scores
        highest = lanes(scores, jnp.maximum)
        highest = jnp.max(highest, axis=1, keepdims=True) if count < 128 else highest
        top = highest if top is None else jnp.maximum(top, highest)
        start += -(-count // 128) * 128
    row_max = jnp.maximum(jnp.max(top, axis=1, keepdims=True), FLOOR)
    if copies:
        copies[1].wait()
    total = jnp.zeros((rows, 1), jnp.float32)
    summed = jnp.zeros((rows, parts[0][1].shape[1]), jnp.float32)
    start = 0
    for keys, values, _ in parts:
        count = keys.shape[0]
        weight = jnp.exp2(score_ref[:, pl.ds(start, count)] - row_max)
        total = total + jnp.sum(lanes(weight, jnp.add), axis=1, keepdims=True)
        summed = summed + jnp.dot(
            weight.astype(jnp.bfloat16), values[...], preferred_element_type=jnp.float32
        )
        start += -(-count // 128) * 128
    return row_max, total, summed


def pack_kernel(slots, table_ref, block_ref, send_ref, near_ref, far_ref):
    _, heads, dev_blocks, _, _ = block_ref.shape
    head_index = lax.axis_index("head")
    sender = lax.axis_index("seq") * heads + head_index
    for block in range(dev_blocks):
        shard = table_ref[sender * dev_blocks + block] // slots
        for head in range(heads):
            for part in range(2):
                send_ref[shard * heads + head, part] = block_ref[part, head, block]
    half = heads // 2
    for offset in range(heads):
        head = head_index ^ offset
        target, at = (near_ref, offset) if offset < half else (far_ref, offset - half)
        for part in range(2):
            target[at, part] = block_ref[part, head].reshape(target.shape[2:])


def resident_kernel(
    scale, len_ref, q_ref, fresh_ref, kv_hbm, out_ref, level_ref, kv_ref, score_ref, sems
):
    resident, length = kv_ref.shape[1], kv_ref.shape[2]
    copies = [
        [
            pltpu.make_async_copy(
                kv_hbm.at[part, request], kv_ref.at[part, request], sems.at[part, request]
            )
            for part in range(2)
        ]
        for request in range(resident)
    ]
    for pair in copies:
        for copy in pair:
            copy.start()
    steps, _, group, depth = q_ref.shape
    rows = steps * group
    diagonal = unit(rows)
    seq_index = lax.axis_index("seq")
    position = seq_index * length + lax.broadcasted_iota(jnp.int32, (1, length), 1)
    for request in range(resident):
        bias = jnp.where(position < len_ref[request], 0.0, MASKED)
        recent = fresh_bias(steps, group, request, resident, 0, seq_index == 0)
        state = attend(
            query_rows(q_ref, request),
            [
                (kv_ref.at[0, request], kv_ref.at[1, request], bias),
                (fresh_ref.at[0, request], fresh_ref.at[1, request], recent),
            ],
            scale,
            score_ref.at[request],
            copies[request],
        )
        mean, level = finish(state, diagonal)
        out_ref[pl.ds(request * rows, rows), :] = mean.astype(jnp.bfloat16)
        level_ref[pl.ds(request, 1), :] = level


def joining_kernel(scale, count, join_ref, q_ref, fresh_ref, res_ref, res_level_ref, *refs):
    sources, (pay_ref, score_ref) = refs[:count], refs[count:]
    steps, requests, group, depth = q_ref.shape
    rows = steps * group
    resident = requests - 1
    diagonal = unit(rows)
    seq_index = lax.axis_index("seq")
    recent = fresh_bias(steps, group, resident, resident, join_ref[0], seq_index == 0)
    parts = [(ref.at[0, 0], ref.at[0, 1], None) for ref in sources]
    parts.append((fresh_ref.at[0, resident], fresh_ref.at[1, resident], recent))
    state = attend(query_rows(q_ref, resident), parts, scale, score_ref)
    mean, level = finish(state, diagonal)
    step = lax.broadcasted_iota(jnp.int32, (rows, depth), 0) // group
    mean = jnp.where(step >= join_ref[0], mean, 0.0)
    pay_ref[pl.ds(0, resident * rows), :] = res_ref[...]
    pay_ref[pl.ds(resident * rows, rows), :] = mean.astype(jnp.bfloat16)
    levels = [res_level_ref[pl.ds(request, 1), :] for request in range(resident)] + [level]
    tail = tail_rows(levels)
    pay_ref[pl.ds(requests * rows, tail.shape[0]), :] = tail


def place_kernel(table_ref, arrived_ref, cache_ref):
    senders = arrived_ref.shape[0]
    slots = cache_ref.shape[1]
    dev_blocks = table_ref.shape[0] // senders
    base = lax.axis_index("seq") * slots

    def settle(sender, carry):
        def look(block, found):
            slot = table_ref[sender * dev_blocks + block] - base
            return jnp.where((slot >= 0) & (slot < slots), slot, found)

        found = lax.fori_loop(0, dev_blocks, look, 0, unroll=True)
        for part in range(2):
            cache_ref[part, found] = arrived_ref[sender, part]
        return carry

    lax.fori_loop(0, senders, settle, 0)


def final_kernel(count, *refs):
    pay_refs, (out_ref,) = refs[:count], refs[count:]
    steps, requests, group, depth = out_ref.shape
    rows = steps * group
    diagonal = unit(rows)
    seq_index = lax.axis_index("seq")
    tail = pl.ds(requests * rows, pay_refs[0].shape[0] - requests * rows)
    tails = [ref[tail, :].astype(jnp.float32) for ref in pay_refs]

    def level_of(rest, request):
        level = rest[request * PIECES : request * PIECES + 1]
        for at in range(request * PIECES + 1, (request + 1) * PIECES):
            level = level + rest[at : at + 1]
        return level

    def in_order(items):
        bit = 1
        while bit < count:
            swap = (seq_index & bit) != 0
            items = [
                jnp.where(swap, items[index ^ bit], items[index]) for index in range(len(items))
            ]
            bit *= 2
        return items

    for request in range(requests):
        levels = [level_of(rest, request) for rest in tails]
        top = functools.reduce(jnp.maximum, levels)
        weights = in_order([jnp.exp2(level - top) for level in levels])
        total = functools.reduce(jnp.add, weights)
        window = pl.ds(request * rows, rows)
        means = in_order([ref[window, :].astype(jnp.float32) for ref in pay_refs])
        result = None
        for mean, weight in zip(means, weights):
            term = mean * to_column(weight / total, diagonal)
            result = term if result is None else result + term
        out_ref[:, request] = result.reshape(steps, group, depth).astype(jnp.bfloat16)


def size_of(array):
    return math.prod(array.shape) * jnp.dtype(array.dtype).itemsize


def call(kernel, out_shape, in_specs, out_specs, flops, scratch=(), grant=0):
    def run(*operands):
        blocks = [
            array
            for array, spec in zip(operands, in_specs)
            if spec.memory_space is pltpu.VMEM
        ]
        blocks += jax.tree.leaves(out_shape)
        held = sum(size_of(array) for array in blocks)
        held += sum(size_of(ref) for ref in scratch if ref.memory_space is pltpu.VMEM)
        return pl.pallas_call(
            kernel,
            out_shape=out_shape,
            in_specs=in_specs,
            out_specs=out_specs,
            scratch_shapes=list(scratch),
            cost_estimate=pl.CostEstimate(
                flops=flops, bytes_accessed=held, transcendentals=0
            ),
            compiler_params=pltpu.CompilerParams(vmem_limit_bytes=max(held + (2 << 20), grant)),
        )(*operands)

    return run


def head_exchange(held, head_count):
    bit = head_count // 2
    while bit:
        pairs = [(index, index ^ bit) for index in range(head_count)]
        kept = [lower for lower, _ in held]
        kept += [lax.ppermute(upper, "head", pairs) for _, upper in held]
        bit //= 2
        if not bit:
            return kept
        held = [(part[:bit], part[bit:]) for part in kept]


def per_device(queries, new_kv, res_kv, prefill_kv, block_table, lengths, join_step):
    seq_count = lax.axis_size("seq")
    head_count = lax.axis_size("head")
    senders = seq_count * head_count
    steps, requests, group, depth = queries.shape
    rows = steps * group
    resident = res_kv.shape[1]
    res_rows = res_kv.shape[2]
    head_total, new_rows = prefill_kv.shape[1:3]
    total_blocks = block_table.shape[0]
    dev_blocks = total_blocks // senders
    block_len = new_rows // dev_blocks
    slots = total_blocks // seq_count
    assert dev_blocks == seq_count and head_total == head_count and rows == depth
    assert seq_count & (seq_count - 1) == 0 and head_count & (head_count - 1) == 0
    scale = LOG2E / math.sqrt(depth)
    bf16, f32 = jnp.bfloat16, jnp.float32
    blocks = prefill_kv.reshape(2, head_total, dev_blocks, block_len, depth)
    fresh = jnp.transpose(new_kv[:, :, :, 0], (0, 2, 1, 3))
    half_shape = jax.ShapeDtypeStruct((head_count // 2, 2, new_rows, depth), bf16)

    outgoing, near, far = call(
        functools.partial(pack_kernel, slots),
        (jax.ShapeDtypeStruct((senders, 2, block_len, depth), bf16), half_shape, half_shape),
        [smem(), vmem()],
        (vmem(), vmem(), vmem()),
        1 << 20,
    )(block_table, blocks)
    sources = head_exchange([(near, far)], head_count)
    arrived = lax.all_to_all(outgoing, ("seq", "head"), split_axis=0, concat_axis=0, tiled=True)

    padded = res_rows + -(-steps // 128) * 128
    res_mean, res_level = call(
        functools.partial(resident_kernel, scale),
        (
            jax.ShapeDtypeStruct((resident * rows, depth), bf16),
            jax.ShapeDtypeStruct((resident, rows), f32),
        ),
        [smem(), vmem(), vmem(), pl.BlockSpec(memory_space=pltpu.HBM)],
        (vmem(), vmem()),
        4 * resident * rows * res_rows * depth,
        [
            pltpu.VMEM((2, resident, res_rows, depth), bf16),
            pltpu.VMEM((resident, rows, padded), f32),
            pltpu.SemaphoreType.DMA((2, resident)),
        ],
        61 << 20,
    )(lengths, queries, fresh, res_kv[:, :, :, 0])

    padded = head_count * new_rows + -(-steps // 128) * 128
    payload = call(
        functools.partial(joining_kernel, scale, len(sources)),
        jax.ShapeDtypeStruct((requests * rows + 16 * -(-requests * PIECES // 16), depth), bf16),
        [smem(), vmem(), vmem(), vmem(), vmem()] + [vmem()] * len(sources),
        vmem(),
        4 * rows * head_count * new_rows * depth,
        [pltpu.VMEM((rows, padded), f32)],
    )(join_step, queries, fresh, res_mean, res_level, *sources)

    shares = [payload]
    for offset in range(1, seq_count):
        pairs = [(index, index ^ offset) for index in range(seq_count)]
        shares.append(lax.ppermute(payload, "seq", pairs))
    attn_out = call(
        functools.partial(final_kernel, seq_count),
        jax.ShapeDtypeStruct((steps, requests, group, depth), bf16),
        [vmem()] * seq_count,
        vmem(),
        1 << 20,
    )(*shares)

    cache = call(
        place_kernel,
        jax.ShapeDtypeStruct((2, slots, block_len, depth), bf16),
        [smem(), vmem()],
        vmem(),
        1 << 20,
    )(block_table, arrived)
    return (attn_out, cache.reshape(2, 1, slots * block_len, depth))


def solution(mesh):
    in_specs = (
        P("groups", None, "head", None),
        P("groups", None, None, "head", None),
        P("groups", None, "seq", "head", None),
        P("groups", None, ("seq", "head"), None),
        P("groups"),
        P("groups"),
        P("groups"),
    )
    out_specs = (P("groups", None, "head", None), P("groups", "head", "seq", None))
    return jax.shard_map(
        per_device, mesh=mesh, in_specs=in_specs, out_specs=out_specs, check_vma=False
    )
```

```python
import functools
import math

import jax
import jax.numpy as jnp
from jax import lax
from jax.experimental import pallas as pl
from jax.experimental.pallas import tpu as pltpu
from jax.sharding import PartitionSpec as P


FLOOR = -1e30
MASKED = -2e30
PIECES = 3
PACK_FLOPS = 1 << 33
LOG2E = math.log2(math.e)


def vmem():
    return pl.BlockSpec(memory_space=pltpu.VMEM)


def smem():
    return pl.BlockSpec(memory_space=pltpu.SMEM)


def query_rows(q_ref, request):
    steps, _, group, depth = q_ref.shape
    wide = q_ref[:, request].astype(jnp.float32)
    return wide.reshape(steps * group, depth).astype(jnp.bfloat16)


def fresh_bias(steps, group, request, resident, joined, owner):
    rows = steps * group
    row_step = lax.broadcasted_iota(jnp.int32, (rows, steps), 0) // group
    key_step = lax.broadcasted_iota(jnp.int32, (rows, steps), 1)
    allowed = (key_step <= row_step) & owner
    if request >= resident:
        allowed = allowed & (key_step >= joined)
    return jnp.where(allowed, 0.0, MASKED)


def unit(rows):
    return lax.broadcasted_iota(jnp.int32, (rows, rows), 0) == lax.broadcasted_iota(
        jnp.int32, (rows, rows), 1
    )


def to_row(column, diagonal):
    return jnp.sum(jnp.where(diagonal, column, 0.0), axis=0, keepdims=True)


def to_column(row, diagonal):
    return jnp.sum(jnp.where(diagonal, row, 0.0), axis=1, keepdims=True)


def split(row):
    parts = []
    rest = row
    for _ in range(PIECES):
        part = rest.astype(jnp.bfloat16).astype(jnp.float32)
        parts.append(part)
        rest = rest - part
    return parts


def finish(state, diagonal):
    row_max, total, summed = state
    safe = jnp.where(total > 0.0, total, 1.0)
    return summed / safe, to_row(row_max + jnp.log2(safe), diagonal)


def tail_rows(levels):
    parts = [part for level in levels for part in split(level)]
    width = parts[0].shape[1]
    count = -(-len(parts) // 16) * 16
    parts.append(jnp.zeros((count - len(parts), width), jnp.float32))
    return jnp.concatenate(parts, axis=0).astype(jnp.bfloat16)


def lanes(wide, op):
    width = wide.shape[1]
    step = min(width, 128)
    out = wide[:, :step]
    for start in range(step, width, step):
        out = op(out, wide[:, start : start + step])
    return out


def attend(query, parts, scale, score_ref):
    rows = query.shape[0]
    top = None
    start = 0
    for keys, _, bias in parts:
        count = keys.shape[0]
        scores = lax.dot_general(
            query, keys[...], (((1,), (1,)), ((), ())), preferred_element_type=jnp.float32
        )
        scores = scores * scale
        if bias is not None:
            scores = scores + bias
        score_ref[:, pl.ds(start, count)] = scores
        highest = lanes(scores, jnp.maximum)
        highest = jnp.max(highest, axis=1, keepdims=True) if count < 128 else highest
        top = highest if top is None else jnp.maximum(top, highest)
        start += -(-count // 128) * 128
    row_max = jnp.maximum(jnp.max(top, axis=1, keepdims=True), FLOOR)
    total = jnp.zeros((rows, 1), jnp.float32)
    summed = jnp.zeros((rows, parts[0][1].shape[1]), jnp.float32)
    start = 0
    for keys, values, _ in parts:
        count = keys.shape[0]
        weight = jnp.exp2(score_ref[:, pl.ds(start, count)] - row_max)
        total = total + jnp.sum(lanes(weight, jnp.add), axis=1, keepdims=True)
        summed = summed + jnp.dot(
            weight.astype(jnp.bfloat16), values[...], preferred_element_type=jnp.float32
        )
        start += -(-count // 128) * 128
    return row_max, total, summed


def pack_kernel(slots, table_ref, block_ref, send_ref):
    _, heads, dev_blocks, _, _ = block_ref.shape
    sender = lax.axis_index("seq") * heads + lax.axis_index("head")
    for block in range(dev_blocks):
        shard = table_ref[sender * dev_blocks + block] // slots
        for head in range(heads):
            for part in range(2):
                send_ref[shard * heads + head, part] = block_ref[part, head, block]


def resident_kernel(scale, len_ref, q_ref, fresh_ref, kv_ref, out_ref, level_ref, score_ref):
    resident, length = kv_ref.shape[1], kv_ref.shape[2]
    steps, _, group, _ = q_ref.shape
    rows = steps * group
    diagonal = unit(rows)
    seq_index = lax.axis_index("seq")
    position = seq_index * length + lax.broadcasted_iota(jnp.int32, (1, length), 1)
    for request in range(resident):
        bias = jnp.where(position < len_ref[request], 0.0, MASKED)
        recent = fresh_bias(steps, group, request, resident, 0, seq_index == 0)
        state = attend(
            query_rows(q_ref, request),
            [
                (kv_ref.at[0, request], kv_ref.at[1, request], bias),
                (fresh_ref.at[0, request], fresh_ref.at[1, request], recent),
            ],
            scale,
            score_ref.at[request],
        )
        mean, level = finish(state, diagonal)
        out_ref[pl.ds(request * rows, rows), :] = mean.astype(jnp.bfloat16)
        level_ref[pl.ds(request, 1), :] = level


def joining_kernel(
    scale, count, join_ref, q_ref, fresh_ref, res_ref, res_level_ref, prefill_ref, *refs
):
    sources, (pay_ref, score_ref) = refs[:count], refs[count:]
    steps, requests, group, depth = q_ref.shape
    rows = steps * group
    resident = requests - 1
    diagonal = unit(rows)
    seq_index = lax.axis_index("seq")
    recent = fresh_bias(steps, group, resident, resident, join_ref[0], seq_index == 0)
    head_index = lax.axis_index("head")
    parts = [(prefill_ref.at[0, head_index], prefill_ref.at[1, head_index], None)]
    parts += [(ref.at[0, 0], ref.at[1, 0], None) for ref in sources]
    parts.append((fresh_ref.at[0, resident], fresh_ref.at[1, resident], recent))
    state = attend(query_rows(q_ref, resident), parts, scale, score_ref)
    mean, level = finish(state, diagonal)
    step = lax.broadcasted_iota(jnp.int32, (rows, depth), 0) // group
    mean = jnp.where(step >= join_ref[0], mean, 0.0)
    pay_ref[pl.ds(0, resident * rows), :] = res_ref[...]
    pay_ref[pl.ds(resident * rows, rows), :] = mean.astype(jnp.bfloat16)
    levels = [res_level_ref[pl.ds(request, 1), :] for request in range(resident)] + [level]
    tail = tail_rows(levels)
    pay_ref[pl.ds(requests * rows, tail.shape[0]), :] = tail


def place_kernel(table_ref, arrived_ref, cache_ref):
    senders = arrived_ref.shape[0]
    slots = cache_ref.shape[1]
    dev_blocks = table_ref.shape[0] // senders
    base = lax.axis_index("seq") * slots

    def settle(sender, carry):
        def look(block, found):
            slot = table_ref[sender * dev_blocks + block] - base
            return jnp.where((slot >= 0) & (slot < slots), slot, found)

        found = lax.fori_loop(0, dev_blocks, look, 0, unroll=True)
        for part in range(2):
            cache_ref[part, found] = arrived_ref[sender, part]
        return carry

    lax.fori_loop(0, senders, settle, 0)


def merged(bit, mine_ref, other_ref, request, requests, rows, diagonal):
    first_here = (lax.axis_index("seq") & bit) == 0
    tail = pl.ds(requests * rows, mine_ref.shape[0] - requests * rows)

    def level_of(ref):
        rest = ref[tail, :].astype(jnp.float32)
        at = request * PIECES
        level = rest[at : at + 1]
        for piece in range(1, PIECES):
            level = level + rest[at + piece : at + piece + 1]
        return level

    def ordered(mine, other):
        return jnp.where(first_here, mine, other), jnp.where(first_here, other, mine)

    first_level, second_level = ordered(level_of(mine_ref), level_of(other_ref))
    top = jnp.maximum(first_level, second_level)
    first_weight = jnp.exp2(first_level - top)
    second_weight = jnp.exp2(second_level - top)
    total = first_weight + second_weight
    window = pl.ds(request * rows, rows)
    first, second = ordered(
        mine_ref[window, :].astype(jnp.float32), other_ref[window, :].astype(jnp.float32)
    )
    mean = first * to_column(first_weight / total, diagonal)
    mean = mean + second * to_column(second_weight / total, diagonal)
    return mean, top + jnp.log2(total)


def merge_kernel(bit, requests, mine_ref, other_ref, out_ref):
    rows = mine_ref.shape[1]
    diagonal = unit(rows)
    levels = []
    for request in range(requests):
        mean, level = merged(bit, mine_ref, other_ref, request, requests, rows, diagonal)
        out_ref[pl.ds(request * rows, rows), :] = mean.astype(jnp.bfloat16)
        levels.append(level)
    tail = tail_rows(levels)
    out_ref[pl.ds(requests * rows, tail.shape[0]), :] = tail


def final_kernel(bit, mine_ref, other_ref, out_ref):
    steps, requests, group, depth = out_ref.shape
    rows = steps * group
    diagonal = unit(rows)
    for request in range(requests):
        mean, _ = merged(bit, mine_ref, other_ref, request, requests, rows, diagonal)
        out_ref[:, request] = mean.reshape(steps, group, depth).astype(jnp.bfloat16)


def size_of(array):
    return math.prod(array.shape) * jnp.dtype(array.dtype).itemsize


def call(kernel, out_shape, in_specs, out_specs, flops, scratch=()):
    def run(*operands):
        blocks = [
            array
            for array, spec in zip(operands, in_specs)
            if spec.memory_space is pltpu.VMEM
        ]
        blocks += jax.tree.leaves(out_shape)
        held = sum(size_of(array) for array in blocks)
        held += sum(size_of(ref) for ref in scratch if ref.memory_space is pltpu.VMEM)
        return pl.pallas_call(
            kernel,
            out_shape=out_shape,
            in_specs=in_specs,
            out_specs=out_specs,
            scratch_shapes=list(scratch),
            cost_estimate=pl.CostEstimate(
                flops=flops, bytes_accessed=held, transcendentals=0
            ),
            compiler_params=pltpu.CompilerParams(vmem_limit_bytes=held + (2 << 20)),
        )(*operands)

    return run


def halves(array, index):
    half = array.shape[1] // 2
    mine = (index // half) % 2
    return [
        lax.dynamic_slice_in_dim(array, place * half, half, 1) for place in (mine, 1 - mine)
    ]


def head_exchange(prefill, head_index, head_count):
    held = [prefill]
    bit = head_count // 2
    while bit:
        pairs = [(index, index ^ bit) for index in range(head_count)]
        split_up = [halves(part, head_index) for part in held]
        sent = [lax.ppermute(other, "head", pairs) for _, other in split_up]
        held = [mine for mine, _ in split_up] + sent
        bit //= 2
    return held[1:]


def per_device(queries, new_kv, res_kv, prefill_kv, block_table, lengths, join_step):
    seq_count = lax.axis_size("seq")
    head_count = lax.axis_size("head")
    senders = seq_count * head_count
    steps, requests, group, depth = queries.shape
    rows = steps * group
    resident = res_kv.shape[1]
    res_rows = res_kv.shape[2]
    head_total, new_rows = prefill_kv.shape[1:3]
    total_blocks = block_table.shape[0]
    dev_blocks = total_blocks // senders
    block_len = new_rows // dev_blocks
    slots = total_blocks // seq_count
    assert dev_blocks == seq_count and head_total == head_count and rows == depth
    assert seq_count & (seq_count - 1) == 0 and head_count & (head_count - 1) == 0
    scale = LOG2E / math.sqrt(depth)
    bf16, f32 = jnp.bfloat16, jnp.float32
    blocks = prefill_kv.reshape(2, head_total, dev_blocks, block_len, depth)
    fresh = jnp.transpose(new_kv[:, :, :, 0], (0, 2, 1, 3))
    sources = head_exchange(prefill_kv, lax.axis_index("head"), head_count)
    outgoing = call(
        functools.partial(pack_kernel, slots),
        jax.ShapeDtypeStruct((senders, 2, block_len, depth), bf16),
        [smem(), vmem()],
        vmem(),
        PACK_FLOPS,
    )(block_table, blocks)
    arrived = lax.all_to_all(
        outgoing, ("seq", "head"), split_axis=0, concat_axis=0, tiled=True
    )

    padded = res_rows + -(-steps // 128) * 128
    res_mean, res_level = call(
        functools.partial(resident_kernel, scale),
        (
            jax.ShapeDtypeStruct((resident * rows, depth), bf16),
            jax.ShapeDtypeStruct((resident, rows), f32),
        ),
        [smem(), vmem(), vmem(), vmem()],
        (vmem(), vmem()),
        4 * resident * rows * res_rows * depth,
        [
            pltpu.VMEM((resident, rows, padded), f32),
        ],
    )(lengths, queries, fresh, res_kv[:, :, :, 0])

    padded = head_count * new_rows + -(-steps // 128) * 128
    payload = call(
        functools.partial(joining_kernel, scale, len(sources)),
        jax.ShapeDtypeStruct((requests * rows + 16 * -(-requests * PIECES // 16), depth), bf16),
        [smem()] + [vmem()] * (5 + len(sources)),
        vmem(),
        4 * rows * head_count * new_rows * depth,
        [pltpu.VMEM((rows, padded), f32)],
    )(join_step, queries, fresh, res_mean, res_level, prefill_kv, *sources)

    bit = 1
    while bit < seq_count:
        pairs = [(index, index ^ bit) for index in range(seq_count)]
        last = 2 * bit >= seq_count
        other = lax.ppermute(payload, "seq", pairs)
        if not last:
            payload = call(
                functools.partial(merge_kernel, bit, requests),
                jax.ShapeDtypeStruct(payload.shape, bf16),
                [vmem(), vmem()],
                vmem(),
                1 << 20,
            )(payload, other)
        bit *= 2
    attn_out = call(
        functools.partial(final_kernel, bit // 2),
        jax.ShapeDtypeStruct((steps, requests, group, depth), bf16),
        [vmem(), vmem()],
        vmem(),
        1 << 20,
    )(payload, other)

    cache = call(
        place_kernel,
        jax.ShapeDtypeStruct((2, slots, block_len, depth), bf16),
        [smem(), vmem()],
        vmem(),
        1 << 20,
    )(block_table, arrived)
    return (attn_out, cache.reshape(2, 1, slots * block_len, depth))


def solution(mesh):
    in_specs = (
        P("groups", None, "head", None),
        P("groups", None, None, "head", None),
        P("groups", None, "seq", "head", None),
        P("groups", None, ("seq", "head"), None),
        P("groups"),
        P("groups"),
        P("groups"),
    )
    out_specs = (P("groups", None, "head", None), P("groups", "head", "seq", None))

    return jax.shard_map(
        per_device, mesh=mesh, in_specs=in_specs, out_specs=out_specs, check_vma=False
    )
```

```python
import functools
import math

import jax
import jax.numpy as jnp
from jax import lax
from jax.experimental import pallas as pl
from jax.experimental.pallas import tpu as pltpu
from jax.sharding import PartitionSpec as P


FLOOR = -1e30
MASKED = -2e30
PIECES = 3
PACK_FLOPS = 1 << 33
LOG2E = math.log2(math.e)


def vmem():
    return pl.BlockSpec(memory_space=pltpu.VMEM)


def smem():
    return pl.BlockSpec(memory_space=pltpu.SMEM)


def hbm():
    return pl.BlockSpec(memory_space=pltpu.HBM)


def in_hbm(array):
    return pltpu.with_memory_space_constraint(array, pltpu.HBM)


def query_rows(q_ref, request):
    steps, _, group, depth = q_ref.shape
    wide = q_ref[:, request].astype(jnp.float32)
    return wide.reshape(steps * group, depth).astype(jnp.bfloat16)


def fresh_bias(steps, group, request, resident, joined, owner):
    rows = steps * group
    row_step = lax.broadcasted_iota(jnp.int32, (rows, steps), 0) // group
    key_step = lax.broadcasted_iota(jnp.int32, (rows, steps), 1)
    allowed = (key_step <= row_step) & owner
    if request >= resident:
        allowed = allowed & (key_step >= joined)
    return jnp.where(allowed, 0.0, MASKED)


def unit(rows):
    return lax.broadcasted_iota(jnp.int32, (rows, rows), 0) == lax.broadcasted_iota(
        jnp.int32, (rows, rows), 1
    )


def to_row(column, diagonal):
    return jnp.sum(jnp.where(diagonal, column, 0.0), axis=0, keepdims=True)


def to_column(row, diagonal):
    return jnp.sum(jnp.where(diagonal, row, 0.0), axis=1, keepdims=True)


def split(row):
    parts = []
    rest = row
    for _ in range(PIECES):
        part = rest.astype(jnp.bfloat16).astype(jnp.float32)
        parts.append(part)
        rest = rest - part
    return parts


def finish(state, diagonal):
    row_max, total, summed = state
    safe = jnp.where(total > 0.0, total, 1.0)
    return summed / safe, to_row(row_max + jnp.log2(safe), diagonal)


def tail_rows(levels):
    parts = [part for level in levels for part in split(level)]
    width = parts[0].shape[1]
    count = -(-len(parts) // 16) * 16
    parts.append(jnp.zeros((count - len(parts), width), jnp.float32))
    return jnp.concatenate(parts, axis=0).astype(jnp.bfloat16)


def lanes(wide, op):
    width = wide.shape[1]
    step = min(width, 128)
    out = wide[:, :step]
    for start in range(step, width, step):
        out = op(out, wide[:, start : start + step])
    return out


def attend(query, parts, scale, score_ref, copies=()):
    if copies:
        copies[0].wait()
    rows = query.shape[0]
    top = None
    start = 0
    for keys, _, bias in parts:
        count = keys.shape[0]
        scores = lax.dot_general(
            query, keys[...], (((1,), (1,)), ((), ())), preferred_element_type=jnp.float32
        )
        scores = scores * scale
        if bias is not None:
            scores = scores + bias
        score_ref[:, pl.ds(start, count)] = scores
        highest = lanes(scores, jnp.maximum)
        highest = jnp.max(highest, axis=1, keepdims=True) if count < 128 else highest
        top = highest if top is None else jnp.maximum(top, highest)
        start += -(-count // 128) * 128
    row_max = jnp.maximum(jnp.max(top, axis=1, keepdims=True), FLOOR)
    if copies:
        copies[1].wait()
    total = jnp.zeros((rows, 1), jnp.float32)
    summed = jnp.zeros((rows, parts[0][1].shape[1]), jnp.float32)
    start = 0
    for keys, values, _ in parts:
        count = keys.shape[0]
        weight = jnp.exp2(score_ref[:, pl.ds(start, count)] - row_max)
        total = total + jnp.sum(lanes(weight, jnp.add), axis=1, keepdims=True)
        summed = summed + jnp.dot(
            weight.astype(jnp.bfloat16), values[...], preferred_element_type=jnp.float32
        )
        start += -(-count // 128) * 128
    return row_max, total, summed


def pack_kernel(
    slots,
    table_hbm,
    block_hbm,
    send_ref,
    far_ref,
    send_near_ref,
    near_ref,
    table_ref,
    sems,
):
    _, heads, dev_blocks, _, _ = block_hbm.shape
    head_index = lax.axis_index("head")
    sender = lax.axis_index("seq") * heads + head_index
    half = heads // 2
    table_copy = pltpu.make_async_copy(table_hbm, table_ref, sems.at[0])
    table_copy.start()
    far = (1 - head_index // half) * half
    quarter = half // 2
    step = (head_index // quarter) % 2 * quarter
    windows = (
        (far, half, far_ref),
        (half - far + quarter - step, quarter, send_near_ref),
        (half - far + step, quarter, near_ref),
    )
    copies = [
        pltpu.make_async_copy(block_hbm.at[:, pl.ds(start, size)], target, sems.at[1 + index])
        for index, (start, size, target) in enumerate(windows)
    ]
    for copy in copies:
        copy.start()
    table_copy.wait()
    for block in range(dev_blocks):
        shard = table_ref[sender * dev_blocks + block] // slots
        for part in range(2):
            copy = pltpu.make_async_copy(
                block_hbm.at[part, :, block],
                send_ref.at[pl.ds(shard * heads, heads), part],
                sems.at[4 + 2 * block + part],
            )
            copy.start()
            copies.append(copy)
    for copy in copies:
        copy.wait()


def resident_kernel(
    scale, len_ref, q_ref, fresh_ref, kv_hbm, out_ref, level_ref, kv_ref, score_ref, sems
):
    resident, length = kv_ref.shape[1], kv_ref.shape[2]
    copies = [
        [
            pltpu.make_async_copy(
                kv_hbm.at[part, request], kv_ref.at[part, request], sems.at[part, request]
            )
            for part in range(2)
        ]
        for request in range(resident)
    ]
    for pair in copies:
        for copy in pair:
            copy.start()
    steps, _, group, _ = q_ref.shape
    rows = steps * group
    diagonal = unit(rows)
    seq_index = lax.axis_index("seq")
    position = seq_index * length + lax.broadcasted_iota(jnp.int32, (1, length), 1)
    for request in range(resident):
        bias = jnp.where(position < len_ref[:, request : request + 1], 0.0, MASKED)
        recent = fresh_bias(steps, group, request, resident, 0, seq_index == 0)
        state = attend(
            query_rows(q_ref, request),
            [
                (kv_ref.at[0, request], kv_ref.at[1, request], bias),
                (fresh_ref.at[0, request], fresh_ref.at[1, request], recent),
            ],
            scale,
            score_ref.at[request],
            copies[request],
        )
        mean, level = finish(state, diagonal)
        out_ref[pl.ds(request * rows, rows), :] = mean.astype(jnp.bfloat16)
        level_ref[pl.ds(request, 1), :] = level


def joining_kernel(scale, count, q_ref, res_ref, res_level_ref, *refs):
    sources, (pay_ref, score_ref) = refs[:count], refs[count:]
    steps, requests, group, _ = q_ref.shape
    rows = steps * group
    resident = requests - 1
    parts = [(ref.at[0, 0], ref.at[1, 0], None) for ref in sources]
    state = attend(query_rows(q_ref, resident), parts, scale, score_ref)
    mean, level = finish(state, unit(rows))
    pay_ref[pl.ds(0, resident * rows), :] = res_ref[...]
    pay_ref[pl.ds(resident * rows, rows), :] = mean.astype(jnp.bfloat16)
    levels = [res_level_ref[pl.ds(request, 1), :] for request in range(resident)] + [level]
    tail = tail_rows(levels)
    pay_ref[pl.ds(requests * rows, tail.shape[0]), :] = tail


def place_kernel(table_ref, arrived_ref, cache_ref):
    senders = arrived_ref.shape[0]
    slots = cache_ref.shape[1]
    dev_blocks = table_ref.shape[0] // senders
    base = lax.axis_index("seq") * slots

    def settle(sender, carry):
        def look(block, found):
            slot = table_ref[sender * dev_blocks + block] - base
            return jnp.where((slot >= 0) & (slot < slots), slot, found)

        found = lax.fori_loop(0, dev_blocks, look, 0, unroll=True)
        for part in range(2):
            cache_ref[part, found] = arrived_ref[sender, part]
        return carry

    lax.fori_loop(0, senders, settle, 0)


def blend(first, second, diagonal):
    top = jnp.maximum(first[1], second[1])
    first_weight = jnp.exp2(first[1] - top)
    second_weight = jnp.exp2(second[1] - top)
    total = first_weight + second_weight
    mean = first[0] * to_column(first_weight / total, diagonal)
    mean = mean + second[0] * to_column(second_weight / total, diagonal)
    return mean, top + jnp.log2(total)


def merged(bit, mine_ref, other_ref, request, requests, rows, diagonal):
    first_here = (lax.axis_index("seq") & bit) == 0
    tail = pl.ds(requests * rows, mine_ref.shape[0] - requests * rows)
    window = pl.ds(request * rows, rows)

    def share(ref):
        rest = ref[tail, :].astype(jnp.float32)
        at = request * PIECES
        level = rest[at : at + 1]
        for piece in range(1, PIECES):
            level = level + rest[at + piece : at + piece + 1]
        return ref[window, :].astype(jnp.float32), level

    pairs = list(zip(share(mine_ref), share(other_ref)))
    first = [jnp.where(first_here, mine, other) for mine, other in pairs]
    second = [jnp.where(first_here, other, mine) for mine, other in pairs]
    return blend(first, second, diagonal)


def store_shares(shares, out_ref):
    rows = shares[0][0].shape[0]
    for request, (mean, _) in enumerate(shares):
        out_ref[pl.ds(request * rows, rows), :] = mean.astype(jnp.bfloat16)
    tail = tail_rows([level for _, level in shares])
    out_ref[pl.ds(len(shares) * rows, tail.shape[0]), :] = tail


def merge_kernel(bit, requests, mine_ref, other_ref, out_ref):
    rows = mine_ref.shape[1]
    diagonal = unit(rows)
    shares = [
        merged(bit, mine_ref, other_ref, request, requests, rows, diagonal)
        for request in range(requests)
    ]
    store_shares(shares, out_ref)


def first_merge_kernel(
    scale, join_ref, q_ref, fresh_ref, mine_ref, other_ref, out_ref, score_ref
):
    steps, requests, group, depth = q_ref.shape
    rows = steps * group
    resident = requests - 1
    diagonal = unit(rows)
    shares = [
        merged(1, mine_ref, other_ref, request, requests, rows, diagonal)
        for request in range(requests)
    ]
    joined = join_ref[0]
    owner = lax.axis_index("seq") < 2
    recent = fresh_bias(steps, group, resident, resident, joined, owner)
    parts = [(fresh_ref.at[0, resident], fresh_ref.at[1, resident], recent)]
    state = attend(query_rows(q_ref, resident), parts, scale, score_ref)
    mean, level = blend(shares[resident], finish(state, diagonal), diagonal)
    step = lax.broadcasted_iota(jnp.int32, (rows, depth), 0) // group
    shares[resident] = jnp.where(step >= joined, mean, 0.0), level
    store_shares(shares, out_ref)


def final_kernel(bit, mine_ref, other_ref, out_ref):
    steps, requests, group, depth = out_ref.shape
    rows = steps * group
    diagonal = unit(rows)
    for request in range(requests):
        mean, _ = merged(bit, mine_ref, other_ref, request, requests, rows, diagonal)
        out_ref[:, request] = mean.reshape(steps, group, depth).astype(jnp.bfloat16)


def size_of(array):
    return math.prod(array.shape) * jnp.dtype(array.dtype).itemsize


def call(kernel, out_shape, in_specs, out_specs, flops, scratch=(), grant=0):
    def run(*operands):
        blocks = [
            array
            for array, spec in zip(operands, in_specs)
            if spec.memory_space is pltpu.VMEM
        ]
        blocks += jax.tree.leaves(out_shape)
        held = sum(size_of(array) for array in blocks)
        held += sum(size_of(ref) for ref in scratch if ref.memory_space is pltpu.VMEM)
        return pl.pallas_call(
            kernel,
            out_shape=out_shape,
            in_specs=in_specs,
            out_specs=out_specs,
            scratch_shapes=list(scratch),
            cost_estimate=pl.CostEstimate(
                flops=flops, bytes_accessed=held, transcendentals=0
            ),
            compiler_params=pltpu.CompilerParams(vmem_limit_bytes=max(held + (2 << 20), grant)),
        )(*operands)

    return run


def halves(array, index):
    half = array.shape[1] // 2
    mine = (index // half) % 2
    return [
        lax.dynamic_slice_in_dim(array, place * half, half, 1) for place in (mine, 1 - mine)
    ]


def head_exchange(far, send_near, near, head_index, head_count):
    def pairs(bit):
        return [(index, index ^ bit) for index in range(head_count)]

    bit = head_count // 2
    arrived = lax.ppermute(far, "head", pairs(bit))
    bit //= 2
    held = [near, lax.ppermute(send_near, "head", pairs(bit))]
    mine, other = halves(arrived, head_index)
    held += [mine, lax.ppermute(other, "head", pairs(bit))]
    bit //= 2
    while bit:
        split_up = [halves(part, head_index) for part in held]
        sent = [lax.ppermute(other, "head", pairs(bit)) for _, other in split_up]
        held = [mine for mine, _ in split_up] + sent
        bit //= 2
    return held


def per_device(queries, new_kv, res_kv, prefill_kv, block_table, lengths, join_step):
    seq_count = lax.axis_size("seq")
    head_count = lax.axis_size("head")
    senders = seq_count * head_count
    steps, requests, group, depth = queries.shape
    rows = steps * group
    resident = res_kv.shape[1]
    res_rows = res_kv.shape[2]
    head_total, new_rows = prefill_kv.shape[1:3]
    total_blocks = block_table.shape[0]
    dev_blocks = total_blocks // senders
    block_len = new_rows // dev_blocks
    slots = total_blocks // seq_count
    assert head_count % 4 == 0 and dev_blocks == seq_count and head_total == head_count and rows == depth
    assert seq_count >= 4 and seq_count & (seq_count - 1) == 0 and head_count & (head_count - 1) == 0
    scale = LOG2E / math.sqrt(depth)
    bf16, f32 = jnp.bfloat16, jnp.float32
    blocks = prefill_kv.reshape(2, head_total, dev_blocks, block_len, depth)
    fresh = jnp.transpose(new_kv[:, :, :, 0], (0, 2, 1, 3))

    def heads_of(count):
        return jax.ShapeDtypeStruct((2, count, dev_blocks, block_len, depth), bf16)

    outgoing, far, send_near, near = call(
        functools.partial(pack_kernel, slots),
        (
            jax.ShapeDtypeStruct((senders, 2, block_len, depth), bf16),
            heads_of(head_count // 2),
            heads_of(head_count // 4),
            heads_of(head_count // 4),
        ),
        [hbm()] * 2,
        [vmem()] * 4,
        PACK_FLOPS,
        [
            pltpu.SMEM((total_blocks,), jnp.int32),
            pltpu.SemaphoreType.DMA((4 + 2 * dev_blocks,)),
        ],
    )(in_hbm(block_table), in_hbm(blocks))
    sources = head_exchange(far, send_near, near, lax.axis_index("head"), head_count)
    sources = [part.reshape(2, 1, new_rows, depth) for part in sources]
    arrived = lax.all_to_all(
        outgoing, ("seq", "head"), split_axis=0, concat_axis=0, tiled=True
    )

    padded = res_rows + -(-steps // 128) * 128
    res_mean, res_level = call(
        functools.partial(resident_kernel, scale),
        (
            jax.ShapeDtypeStruct((resident * rows, depth), bf16),
            jax.ShapeDtypeStruct((resident, rows), f32),
        ),
        [vmem()] * 3 + [hbm()],
        (vmem(), vmem()),
        4 * resident * rows * res_rows * depth,
        [
            pltpu.VMEM((2, resident, res_rows, depth), bf16),
            pltpu.VMEM((resident, rows, padded), f32),
            pltpu.SemaphoreType.DMA((2, resident)),
        ],
    )(lengths.reshape(1, requests), queries, fresh, in_hbm(res_kv[:, :, :, 0]))

    payload = call(
        functools.partial(joining_kernel, scale, len(sources)),
        jax.ShapeDtypeStruct((requests * rows + 16 * -(-requests * PIECES // 16), depth), bf16),
        [vmem()] * (3 + len(sources)),
        vmem(),
        4 * rows * head_count * new_rows * depth,
        [pltpu.VMEM((rows, head_count * new_rows), f32)],
    )(queries, res_mean, res_level, *sources)

    bit = 1
    while bit < seq_count:
        pairs = [(index, index ^ bit) for index in range(seq_count)]
        last = 2 * bit >= seq_count
        other = lax.ppermute(payload, "seq", pairs)
        if bit == 1:
            payload = call(
                functools.partial(first_merge_kernel, scale),
                jax.ShapeDtypeStruct(payload.shape, bf16),
                [smem()] + [vmem()] * 4,
                vmem(),
                1 << 20,
                [pltpu.VMEM((rows, 128), f32)],
            )(join_step, queries, fresh, payload, other)
        elif not last:
            payload = call(
                functools.partial(merge_kernel, bit, requests),
                jax.ShapeDtypeStruct(payload.shape, bf16),
                [vmem(), vmem()],
                vmem(),
                1 << 20,
            )(payload, other)
        bit *= 2
    attn_out = call(
        functools.partial(final_kernel, bit // 2),
        jax.ShapeDtypeStruct((steps, requests, group, depth), bf16),
        [vmem(), vmem()],
        vmem(),
        1 << 20,
    )(payload, other)

    cache = call(
        place_kernel,
        jax.ShapeDtypeStruct((2, slots, block_len, depth), bf16),
        [smem(), vmem()],
        vmem(),
        1 << 20,
    )(block_table, arrived)
    return (attn_out, cache.reshape(2, 1, slots * block_len, depth))


def solution(mesh):
    in_specs = (
        P("groups", None, "head", None),
        P("groups", None, None, "head", None),
        P("groups", None, "seq", "head", None),
        P("groups", None, ("seq", "head"), None),
        P("groups"),
        P("groups"),
        P("groups"),
    )
    out_specs = (P("groups", None, "head", None), P("groups", "head", "seq", None))

    return jax.shard_map(
        per_device, mesh=mesh, in_specs=in_specs, out_specs=out_specs, check_vma=False
    )
```
